128 devices in a mesh: grid: 4 (over y), ens: 32 (over x, z, core).
Axes of the slice: x: 4, y: 4, z: 4, core: 2. Of those that a mesh axis runs over, the one named last changes fastest.
Arguments:
- snapshots: bfloat16 [4096, 32768], P('ens', 'grid'), may hold values from -32 to 32
- tile_mask: int32 [64, 5], P('grid'), may hold values from 0 to 1, as said below
- kernels: bfloat16 [5, 512, 512], replicated, may hold values from -2 to 2
- test_matrix: bfloat16 [4096, 256], P('ens'), may hold values from -0.09375 to 0.09375
Outputs:
- basis: float32 [32768, 256], P(('grid', 'ens'))
- coefficients: float32 [4096, 256], P('ens')
The draws below stay inside these ranges and needn't reach their ends.
Inputs may be any that keep to these rules, and one draw needn't show every extreme that they name: `tile_mask`: the middle diagonal (index 2) is present in every tile row.
All inputs are finite; a program needn't handle non-finite values.
Results may differ from the reference program's by a relative error of at most 0.0033.
Values may be sent and summed in bfloat16 or wider, within the bound.
A program may use at most 64 MiB of HBM per device.

```python
import math
import jax
import jax.numpy as jnp
from jax import lax

TILE = 512
DIAGS = 5
RANK = 256
SCEN = 4096
NC = 32768
NT = 64


def draw_snapshots(key, part):
    key_base = jax.random.fold_in(key, 11)
    key_noise = jax.random.fold_in(key, 23)
    key_left = jax.random.fold_in(key, 37)
    key_right = jax.random.fold_in(key, 41)
    base = jnp.clip(jax.random.normal(key_base, (NC,), jnp.float32), -4.0, 4.0)
    ramp = 0.5 + jnp.arange(SCEN).astype(jnp.float32) / SCEN
    levels = 2.0 ** (1.0 - jnp.arange(RANK).astype(jnp.float32) / (RANK - 1))
    rising = 1.0 + 2.0 * jnp.arange(NC).astype(jnp.float32) / NC
    left = jax.random.normal(key_left, (SCEN, RANK), jnp.float32) * levels[None, :]
    right = jax.random.normal(key_right, (RANK, NC), jnp.float32) / jnp.sqrt(jnp.float32(RANK))
    planted = jnp.clip(jnp.dot(left, right, precision=lax.Precision.HIGHEST), -8.0, 8.0)
    noise = jnp.clip(jax.random.normal(key_noise, (SCEN, NC), jnp.float32), -5.0, 5.0) * 0.1
    return (ramp[:, None] * base[None, :] + (planted + noise) * rising[None, :]).astype(jnp.bfloat16)


def draw_tile_mask(key, part):
    picks = jax.random.randint(jax.random.fold_in(key, 5), (NT, DIAGS), 0, 4)
    present = (picks > 0).astype(jnp.int32)
    middle = jnp.arange(DIAGS)[None, :] == DIAGS // 2
    return jnp.where(middle, 1, present).astype(jnp.int32)


def draw_kernels(key, part):
    sigma = 0.25 / jnp.sqrt(jnp.float32(DIAGS * TILE))
    noise = jnp.clip(jax.random.normal(jax.random.fold_in(key, 7), (DIAGS, TILE, TILE), jnp.float32), -5.0, 5.0) * sigma
    eye = (jnp.arange(TILE)[:, None] == jnp.arange(TILE)[None, :]).astype(jnp.float32)
    middle = (jnp.arange(DIAGS) == DIAGS // 2).astype(jnp.float32)
    return (noise + middle[:, None, None] * eye[None, :, :]).astype(jnp.bfloat16)


def steps_of(own_key, shape, pieces, low, top_value):
    def one(position, shards_of):
        steps = jax.random.uniform(jax.random.fold_in(jax.random.fold_in(own_key, 6), position), (shards_of,), jnp.float32, low / len(pieces), top_value / len(pieces))
        return jnp.repeat(jnp.exp(steps), shape[position] // shards_of).reshape((-1,) + (1,) * (len(shape) - position - 1))

    loudness = one(*pieces[0])
    for cut in pieces[1:]:
        loudness = loudness * one(*cut)
    return loudness


def scatter_about(rng, dims, spread, reach, cuts=(), kind=jnp.bfloat16):
    level = steps_of(rng, dims, cuts, -0.22, 0.18) if cuts else 1.0
    values = jax.random.normal(rng, dims, jnp.float32) * spread * level
    return jnp.minimum(jnp.maximum(values, -reach), reach).astype(kind)


def setup_inputs(seed: int = 0) -> dict:
    seeds = jax.random.split(jax.random.key(seed), 5)
    return {
        "snapshots": draw_snapshots(jax.random.fold_in(seeds[4], 71), 0),
        "tile_mask": draw_tile_mask(jax.random.fold_in(seeds[4], 71), 0),
        "kernels": draw_kernels(jax.random.fold_in(seeds[4], 71), 0),
        "test_matrix": scatter_about(seeds[3], (SCEN, RANK), SCEN ** -0.5, 0.09375, ((0, 32),)),
    }


def localize(anomaly, tile_mask, kernels):
    half = DIAGS // 2
    padded = jnp.pad(anomaly, ((0, 0), (half * TILE, half * TILE)))
    tiles = padded.reshape(SCEN, NT + 2 * half, TILE)
    total = jnp.zeros((SCEN, NT, TILE), jnp.float32)
    for diag in range(DIAGS):
        prod = jnp.einsum('sit,tu->siu', tiles[:, diag:diag + NT].astype(jnp.float32), kernels[diag].astype(jnp.float32))
        total = total + prod * tile_mask[:, diag].astype(jnp.float32)[None, :, None]
    return total.reshape(SCEN, NC).astype(jnp.bfloat16)

def span_of(fields, mixing):
    return lax.dot_general(fields.astype(jnp.float32), mixing.astype(jnp.float32), (((0,), (0,)), ((), ())), preferred_element_type=jnp.float32)

def orthonormal(span):
    gram = jnp.dot(span.T, span, precision=lax.Precision.HIGHEST)
    lower = jnp.linalg.cholesky(gram)
    return jax.scipy.linalg.solve_triangular(lower, span.T, lower=True).T

def reference(snapshots, tile_mask, kernels, test_matrix):
    means = lax.optimization_barrier(jnp.sum(snapshots, axis=0, dtype=jnp.float32)) / SCEN
    anomaly = (snapshots.astype(jnp.float32) - means[None, :]).astype(jnp.bfloat16)
    fields = localize(anomaly, tile_mask, kernels)
    first_basis = orthonormal(span_of(fields, test_matrix)).astype(jnp.bfloat16)
    weights = jnp.dot(fields.astype(jnp.float32), first_basis.astype(jnp.float32), preferred_element_type=jnp.float32).astype(jnp.bfloat16)
    second_basis = orthonormal(span_of(fields, weights))
    basis = second_basis * math.sqrt(NC)
    coefficients = jnp.dot(fields.astype(jnp.float32), second_basis.astype(jnp.bfloat16).astype(jnp.float32), preferred_element_type=jnp.float32) * math.sqrt(RANK / NC)
    return (basis, coefficients)
```

```python
import functools
import math

import jax
import jax.numpy as jnp
from jax import lax
from jax.experimental import pallas as pl
from jax.experimental.pallas import tpu as pltpu
from jax.sharding import PartitionSpec as P

MESH = pl.DeviceIdType.MESH
HIGHEST = lax.Precision.HIGHEST
VMEM = pl.BlockSpec(memory_space=pltpu.VMEM)
ANY = pl.BlockSpec(memory_space=pl.ANY)
NX, NZ, NCORE, NY = 4, 4, 2, 4
PLANE = NX * NZ * NCORE
LIMIT = 60 * 1024 * 1024


def place():
    me = lax.axis_index("ens")
    return me, me // (NZ * NCORE), (me // NCORE) % NZ, me % NCORE


def greet(peers):
    barrier = pltpu.get_barrier_semaphore()
    for peer in peers:
        pl.semaphore_signal(barrier, inc=1, device_id=peer, device_id_type=MESH)
    pl.semaphore_wait(barrier, len(peers))


def greet_plane(me, others=()):
    barrier = pltpu.get_barrier_semaphore()

    def one(k, carry):
        peer = (me + k) % PLANE
        pl.semaphore_signal(barrier, inc=1, device_id={"ens": peer}, device_id_type=MESH)
        return carry

    lax.fori_loop(1, PLANE, one, 0)
    for peer in others:
        pl.semaphore_signal(barrier, inc=1, device_id=peer, device_id_type=MESH)
    pl.semaphore_wait(barrier, PLANE - 1 + len(others))


def remote(src, dst, send, recv, peer):
    return pltpu.make_async_remote_copy(
        src_ref=src, dst_ref=dst, send_sem=send, recv_sem=recv, device_id=peer, device_id_type=MESH
    )


def each(low, high, body):
    def step(k, carry):
        body(k)
        return carry

    lax.fori_loop(low, high, step, 0)


def exchange_kernel(local_ref, means_ref, out_ref, all_means_ref, own_sem, send, recv, msend, mrecv):
    me = lax.axis_index("ens")
    width = out_ref.shape[2]
    greet_plane(me)

    def columns(owner):
        return pl.ds(pl.multiple_of(owner * width, width), width)

    def copies(k):
        peer = {"ens": (me + k) % PLANE}
        cols = columns((me + k) % PLANE)
        return (
            remote(means_ref.at[:, cols], all_means_ref.at[me], msend.at[k], mrecv.at[k], peer),
            remote(local_ref.at[:, cols], out_ref.at[me], send.at[k], recv.at[k], peer),
        )

    def start(k):
        for copy in copies(k):
            copy.start()

    each(1, PLANE, start)
    own = (
        pltpu.make_async_copy(local_ref.at[:, columns(me)], out_ref.at[me], own_sem.at[0]),
        pltpu.make_async_copy(means_ref.at[:, columns(me)], all_means_ref.at[me], own_sem.at[1]),
    )
    for copy in own:
        copy.start()
    for copy in own:
        copy.wait()

    def finish(k):
        for copy in copies(k):
            copy.wait()

    each(1, PLANE, finish)


def exchange(local, means):
    scen, cells = local.shape
    width = cells // PLANE
    return pl.pallas_call(
        exchange_kernel,
        out_shape=(
            jax.ShapeDtypeStruct((PLANE, scen, width), local.dtype),
            jax.ShapeDtypeStruct((PLANE, means.shape[0], width), means.dtype),
        ),
        in_specs=[VMEM, VMEM],
        out_specs=(VMEM, VMEM),
        scratch_shapes=[pltpu.SemaphoreType.DMA((2,))] + [pltpu.SemaphoreType.DMA((PLANE,))] * 4,
        compiler_params=pltpu.CompilerParams(collective_id=0, has_side_effects=True, vmem_limit_bytes=LIMIT),
        name="exchange",
    )(local, means)


def gather_kernel(own_ref, out_ref, own_sem, send, recv, core_send, core_recv):
    me, x, z, c = place()
    half = own_ref.shape[1] // 2
    xs = [((x + k) % NX) for k in range(1, NX)]
    zs = [((z + k) % NZ) for k in range(1, NZ)]
    xpeers = [{"ens": v * NZ * NCORE + z * NCORE + c} for v in xs]
    zpeers = [{"ens": x * NZ * NCORE + v * NCORE + c} for v in zs]
    twin = {"ens": me + 1 - 2 * c}
    greet(xpeers + zpeers + [twin])
    left, right = pl.ds(0, half), pl.ds(half, half)
    first = []
    for k in range(NX - 1):
        first.append(remote(own_ref.at[:, left], out_ref.at[x, z, c, :, left], send.at[0, k], recv.at[0, k], xpeers[k]))
        first.append(remote(own_ref.at[:, right], out_ref.at[x, z, c, :, right], send.at[1, k], recv.at[1, k], zpeers[k]))
    for copy in first:
        copy.start()
    mine = pltpu.make_async_copy(own_ref, out_ref.at[x, z, c], own_sem)
    mine.start()
    mine.wait()
    for copy in first:
        copy.wait()
    second = []
    for k in range(NX - 1):
        second.append(remote(out_ref.at[:, z, c, :, left], out_ref.at[:, z, c, :, left], send.at[2, k], recv.at[2, k], zpeers[k]))
        second.append(remote(out_ref.at[x, :, c, :, right], out_ref.at[x, :, c, :, right], send.at[3, k], recv.at[3, k], xpeers[k]))
    for copy in second:
        copy.start()
    for copy in second:
        copy.wait()
    swap = remote(out_ref.at[:, :, c], out_ref.at[:, :, c], core_send, core_recv, twin)
    swap.start()
    swap.wait()


def gather(own, number):
    rows, cols = own.shape
    out = pl.pallas_call(
        gather_kernel,
        out_shape=jax.ShapeDtypeStruct((NX, NZ, NCORE, rows, cols), own.dtype),
        in_specs=[VMEM],
        out_specs=VMEM,
        scratch_shapes=[
            pltpu.SemaphoreType.DMA,
            pltpu.SemaphoreType.DMA((4, NX - 1)),
            pltpu.SemaphoreType.DMA((4, NX - 1)),
            pltpu.SemaphoreType.DMA,
            pltpu.SemaphoreType.DMA,
        ],
        compiler_params=pltpu.CompilerParams(collective_id=number, has_side_effects=True, vmem_limit_bytes=LIMIT),
        name="gather_rows",
    )(own)
    return out.reshape(PLANE * rows, cols)


def reduce_kernel(
    part_ref, gram_ref, rows_ref, out_gram_ref,
    from_twin, both, over_x, over_z, late_z, late_x, stage0, stage1, plane_sum, from_y,
    gram_in, gram_rows, gram_y,
    twin_send, twin_recv, send, recv, ysend, yrecv, gsend, grecv, gysend, gyrecv, bsend, brecv,
):
    me, x, z, c = place()
    y = lax.axis_index("grid")
    half = rows_ref.shape[1] // 2
    left, right = pl.ds(0, half), pl.ds(half, half)
    xs = [((x + k) % NX) for k in range(1, NX)]
    zs = [((z + k) % NZ) for k in range(1, NZ)]
    xpeers = [{"ens": v * NZ * NCORE + z * NCORE + c} for v in xs]
    zpeers = [{"ens": x * NZ * NCORE + v * NCORE + c} for v in zs]
    ypeers = [{"grid": (y + k) % NY} for k in range(1, NY)]
    twin = {"ens": me + 1 - 2 * c}
    greet_plane(me, ypeers)

    def gram_copy(k):
        peer = (me + k) % PLANE
        return remote(gram_ref.at[peer], gram_in.at[me], gsend.at[k], grecv.at[k], {"ens": peer})

    each(1, PLANE, lambda k: gram_copy(k).start())
    order = xs + [x]
    halves = [
        remote(part_ref.at[v, :, 1 - c], from_twin.at[v], twin_send.at[i], twin_recv.at[i], twin)
        for i, v in enumerate(order)
    ]
    for copy in halves:
        copy.start()
    x_first = []
    for i, v in enumerate(order):
        halves[i].wait()
        both[v] = part_ref[v, :, c] + from_twin[v]
        if i < NX - 1:
            copy = remote(both.at[v, :, :, left], over_x.at[i], send.at[0, i], recv.at[0, i], xpeers[i])
            copy.start()
            x_first.append(copy)
    z_first = []
    for i, v in enumerate(zs):
        copy = remote(both.at[:, v, :, right], over_z.at[i], send.at[1, i], recv.at[1, i], zpeers[i])
        copy.start()
        z_first.append(copy)
    gram_in[me] = gram_ref[me]
    each(1, PLANE, lambda k: gram_copy(k).wait())
    gram_rows[...] = jnp.sum(gram_in[...], axis=0)
    gram_over_y = [
        remote(gram_rows, gram_y.at[k], gysend.at[k], gyrecv.at[k], ypeers[k]) for k in range(NY - 1)
    ]
    for copy in gram_over_y:
        copy.start()
    for copy in gram_over_y:
        copy.wait()
    own_rows = gram_rows[...] + jnp.sum(gram_y[...], axis=0)
    out_gram_ref[me] = own_rows

    def gram_back(k):
        return remote(out_gram_ref.at[me], out_gram_ref.at[me], bsend.at[k], brecv.at[k], {"ens": (me + k) % PLANE})

    each(1, PLANE, lambda k: gram_back(k).start())
    for copy in x_first:
        copy.wait()
    stage0[...] = both[x, :, :, 0:half] + over_x[0] + over_x[1] + over_x[2]
    second = [
        remote(stage0.at[v], late_z.at[i], send.at[2, i], recv.at[2, i], zpeers[i]) for i, v in enumerate(zs)
    ]
    for copy in second:
        copy.start()
    for copy in z_first:
        copy.wait()
    stage1[...] = both[:, z, :, half:] + over_z[0] + over_z[1] + over_z[2]
    third = [
        remote(stage1.at[v], late_x.at[i], send.at[3, i], recv.at[3, i], xpeers[i]) for i, v in enumerate(xs)
    ]
    for copy in third:
        copy.start()
    for copy in second:
        copy.wait()
    plane_sum[:, 0:half] = stage0[z] + late_z[0] + late_z[1] + late_z[2]
    for copy in third:
        copy.wait()
    plane_sum[:, half:] = stage1[x] + late_x[0] + late_x[1] + late_x[2]
    over_y = [remote(plane_sum, from_y.at[k], ysend.at[k], yrecv.at[k], ypeers[k]) for k in range(NY - 1)]
    for copy in over_y:
        copy.start()
    for copy in over_y:
        copy.wait()
    rows_ref[...] = plane_sum[...] + from_y[0] + from_y[1] + from_y[2]
    each(1, PLANE, lambda k: gram_back(k).wait())


def reduce_sums(part, gram, number):
    total, cols = part.shape
    rows = total // PLANE
    half = cols // 2
    grows = gram.shape[0] // PLANE
    f32 = jnp.float32
    dma = pltpu.SemaphoreType.DMA
    out, summed = pl.pallas_call(
        reduce_kernel,
        out_shape=(
            jax.ShapeDtypeStruct((rows, cols), f32),
            jax.ShapeDtypeStruct((PLANE, grows, cols), f32),
        ),
        in_specs=[VMEM, VMEM],
        out_specs=(VMEM, VMEM),
        scratch_shapes=[
            pltpu.VMEM((NX, NZ, rows, cols), f32),
            pltpu.VMEM((NX, NZ, rows, cols), f32),
            pltpu.VMEM((NX - 1, NZ, rows, half), f32),
            pltpu.VMEM((NZ - 1, NX, rows, half), f32),
            pltpu.VMEM((NZ - 1, rows, half), f32),
            pltpu.VMEM((NX - 1, rows, half), f32),
            pltpu.VMEM((NZ, rows, half), f32),
            pltpu.VMEM((NX, rows, half), f32),
            pltpu.VMEM((rows, cols), f32),
            pltpu.VMEM((NY - 1, rows, cols), f32),
            pltpu.VMEM((PLANE, grows, cols), f32),
            pltpu.VMEM((grows, cols), f32),
            pltpu.VMEM((NY - 1, grows, cols), f32),
            dma((NX,)), dma((NX,)), dma((4, NX - 1)), dma((4, NX - 1)), dma((NY - 1,)), dma((NY - 1,)),
            dma((PLANE,)), dma((PLANE,)), dma((NY - 1,)), dma((NY - 1,)), dma((PLANE,)), dma((PLANE,)),
        ],
        compiler_params=pltpu.CompilerParams(collective_id=number, has_side_effects=True, vmem_limit_bytes=LIMIT),
        name="reduce_sums",
    )(part.reshape(NX, NZ, NCORE, rows, cols), gram.reshape(PLANE, grows, cols))
    return out, summed.reshape(gram.shape)


BLOCK = 64


def eliminated(m):
    size = m.shape[0]
    row = lax.broadcasted_iota(jnp.int32, m.shape, 0)
    col = lax.broadcasted_iota(jnp.int32, m.shape, 1)
    for j in range(0, size, 2):
        c0 = jnp.broadcast_to(m[:, j : j + 1], m.shape)
        c1 = jnp.broadcast_to(m[:, j + 1 : j + 2], m.shape)
        r0 = m[j : j + 1, :]
        r1 = m[j + 1 : j + 2, :]
        d0 = c0[j : j + 1, :]
        e = c0[j + 1 : j + 2, :]
        f = c1[j + 1 : j + 2, :]
        ratio = e / d0
        d1 = f - e * ratio
        u0 = r0 / d0
        u1 = (r1 - ratio * r0) / d1
        c1 = jnp.where(row > j + 1, c1 - c0 * ratio, 0.0)
        c0 = jnp.where(row > j, c0, 0.0)
        m = m - c0 * u0 - c1 * u1
    diag = jnp.sum(jnp.where(row == col, m, 0.0), axis=1, keepdims=True)
    return m * (1.0 / jnp.sqrt(diag))


def inverse_factor_kernel(gram_ref, out_ref, work):
    n = gram_ref.shape[0]
    work[:, 0:n] = gram_ref[...]
    row = lax.broadcasted_iota(jnp.int32, (n, n), 0)
    col = lax.broadcasted_iota(jnp.int32, (n, n), 1)
    work[:, n:] = jnp.where(row == col, 1.0, 0.0)
    brow = lax.broadcasted_iota(jnp.int32, (BLOCK, BLOCK), 0)
    bcol = lax.broadcasted_iota(jnp.int32, (BLOCK, BLOCK), 1)
    unit = jnp.where(brow == bcol, 1.0, 0.0)
    for low in range(0, n, BLOCK):
        high = low + BLOCK
        block = work[low:high, low:high]
        inv = eliminated(jnp.concatenate([block, unit], axis=1))[:, BLOCK:]
        scaled = jnp.dot(inv, work[low:high, :], precision=HIGHEST, preferred_element_type=jnp.float32)
        out_ref[low:high, :] = scaled[:, n:]
        if high < n:
            lower = scaled[:, high:n]
            update = lax.dot_general(
                lower, scaled, (((0,), (0,)), ((), ())), precision=HIGHEST, preferred_element_type=jnp.float32
            )
            work[high:, :] = work[high:, :] - update


def inverse_factor(gram):
    n = gram.shape[0]
    return pl.pallas_call(
        inverse_factor_kernel,
        out_shape=jax.ShapeDtypeStruct((n, n), jnp.float32),
        in_specs=[VMEM],
        out_specs=VMEM,
        scratch_shapes=[pltpu.VMEM((n, 2 * n), jnp.float32)],
        name="inverse_factor",
    )(gram)


def halos(block, width):
    count = lax.axis_size("grid")
    forward = [(i, i + 1) for i in range(count - 1)]
    backward = [(target, source) for source, target in forward]
    low = lax.ppermute(block[:, block.shape[1] - width :], "grid", forward)
    high = lax.ppermute(block[:, :width], "grid", backward)
    return jnp.concatenate([low, block, high], axis=1)


def localize(snapshots, tile_mask, kernels):
    diags = kernels.shape[0]
    half = diags // 2
    tile_width = kernels.shape[1]
    scen_dev = snapshots.shape[0]
    tiles_dev = tile_mask.shape[0]
    tiles = halos(snapshots, half * tile_width).reshape(scen_dev, tiles_dev + 2 * half, tile_width)
    total = jnp.zeros((scen_dev, tiles_dev, tile_width), jnp.float32)
    for diag in range(diags):
        prod = jnp.einsum(
            "sit,tu->siu",
            tiles[:, diag : diag + tiles_dev],
            kernels[diag],
            preferred_element_type=jnp.float32,
        )
        total = total + prod * tile_mask[:, diag].astype(jnp.float32)[None, :, None]
    return total.reshape(scen_dev, tiles_dev * tile_width)


def product(fields, span):
    high = span.astype(jnp.bfloat16)
    low = (span - high.astype(jnp.float32)).astype(jnp.bfloat16)
    both = jnp.dot(fields, jnp.concatenate([high, low], axis=1), preferred_element_type=jnp.float32)
    cols = span.shape[1]
    return both[:, :cols] + both[:, cols:]


def span_of(fields, mixing):
    return lax.dot_general(fields, mixing, (((0,), (0,)), ((), ())), preferred_element_type=jnp.float32)


def gram_of(span):
    return lax.dot_general(span, span, (((0,), (0,)), ((), ())), precision=HIGHEST)


def times_inverse_transposed(rows, inverse):
    return lax.dot_general(rows, inverse, (((1,), (1,)), ((), ())), precision=HIGHEST)


def per_device(snapshots, tile_mask, kernels, test_matrix):
    total_cells = snapshots.shape[1] * lax.axis_size("grid")
    rank_width = test_matrix.shape[1]
    mixing = gather(test_matrix, 1)
    total = localize(snapshots, tile_mask, kernels)
    block_means = jnp.mean(total, axis=0, keepdims=True)
    blocks, all_means = exchange(
        (total - block_means).astype(jnp.bfloat16), jnp.broadcast_to(block_means, (8, total.shape[1]))
    )
    all_means = all_means[:, :1]
    shift = all_means - jnp.mean(all_means, axis=0, keepdims=True)
    fields = (blocks.astype(jnp.float32) + shift).astype(jnp.bfloat16)
    fields = fields.reshape(-1, fields.shape[2])

    first_span = span_of(fields, mixing)
    rows, gram = reduce_sums(product(fields, first_span), gram_of(first_span), 2)
    weights = times_inverse_transposed(rows, inverse_factor(gram)).astype(jnp.bfloat16)
    second_span = span_of(fields, gather(weights, 3))
    rows, gram = reduce_sums(product(fields, second_span), gram_of(second_span), 4)
    inverse = inverse_factor(gram)
    basis = times_inverse_transposed(second_span, inverse) * math.sqrt(total_cells)
    coefficients = times_inverse_transposed(rows, inverse) * math.sqrt(rank_width / total_cells)
    return (basis, coefficients)


def solution(mesh):
    return jax.shard_map(
        per_device,
        mesh=mesh,
        in_specs=(P("ens", "grid"), P("grid", None), P(), P("ens", None)),
        out_specs=(P(("grid", "ens"), None), P("ens", None)),
        check_vma=False,
    )
```

```python
import functools
import math

import jax
import jax.numpy as jnp
from jax import lax
from jax.experimental import pallas as pl
from jax.experimental.pallas import tpu as pltpu
from jax.sharding import PartitionSpec as P

MESH = pl.DeviceIdType.MESH
HIGHEST = lax.Precision.HIGHEST
VMEM = pl.BlockSpec(memory_space=pltpu.VMEM)
ANY = pl.BlockSpec(memory_space=pl.ANY)
NX, NZ, NCORE, NY = 4, 4, 2, 4
PLANE = NX * NZ * NCORE
LIMIT = 60 * 1024 * 1024


def place():
    me = lax.axis_index("ens")
    return me, me // (NZ * NCORE), (me // NCORE) % NZ, me % NCORE


def greet(peers):
    barrier = pltpu.get_barrier_semaphore()
    for peer in peers:
        pl.semaphore_signal(barrier, inc=1, device_id=peer, device_id_type=MESH)
    pl.semaphore_wait(barrier, len(peers))


def greet_plane(me, others=()):
    barrier = pltpu.get_barrier_semaphore()

    def one(k, carry):
        peer = (me + k) % PLANE
        pl.semaphore_signal(barrier, inc=1, device_id={"ens": peer}, device_id_type=MESH)
        return carry

    lax.fori_loop(1, PLANE, one, 0)
    for peer in others:
        pl.semaphore_signal(barrier, inc=1, device_id=peer, device_id_type=MESH)
    pl.semaphore_wait(barrier, PLANE - 1 + len(others))


def remote(src, dst, send, recv, peer):
    return pltpu.make_async_remote_copy(
        src_ref=src, dst_ref=dst, send_sem=send, recv_sem=recv, device_id=peer, device_id_type=MESH
    )


def each(low, high, body):
    def step(k, carry):
        body(k)
        return carry

    lax.fori_loop(low, high, step, 0)


def spread_kernel(
    snap_ref, mask_ref, kernels_ref, mix_ref,
    out_ref, all_means_ref, mixing_ref,
    padded, blocks, means,
    load_sem, own_sem, hsend, hrecv, send, recv, msend, mrecv, tsend, trecv, twin_send, twin_recv,
):
    me, x, z, c = place()
    y = lax.axis_index("grid")
    chip = me // NCORE
    diags, tile, _ = kernels_ref.shape
    halo = (diags // 2) * tile
    scen, cells = snap_ref.shape
    tiles = cells // tile
    width = out_ref.shape[2]
    inner = tiles - 2 * (diags // 2)
    up, down = {"grid": (y + 1) % NY}, {"grid": (y + NY - 1) % NY}
    greet_plane(me, (up, down))

    load = pltpu.make_async_copy(snap_ref, padded.at[:, pl.ds(halo, cells)], load_sem)
    load.start()
    over_y = (
        remote(snap_ref.at[:, pl.ds(cells - halo, halo)], padded.at[:, pl.ds(0, halo)], hsend.at[0], hrecv.at[0], up),
        remote(snap_ref.at[:, pl.ds(0, halo)], padded.at[:, pl.ds(halo + cells, halo)], hsend.at[1], hrecv.at[1], down),
    )
    for copy in over_y:
        copy.start()

    half = mix_ref.shape[1] // 2
    left, right = pl.ds(0, half), pl.ds(half, half)
    xpeers = [{"ens": ((x + k) % NX) * NZ * NCORE + z * NCORE + c} for k in range(1, NX)]
    zpeers = [{"ens": x * NZ * NCORE + ((z + k) % NZ) * NCORE + c} for k in range(1, NZ)]
    twin = {"ens": me + 1 - 2 * c}
    first, second = [], []
    for k in range(NX - 1):
        first.append(remote(mix_ref.at[:, left], mixing_ref.at[x, z, c, :, left], tsend.at[0, k], trecv.at[0, k], xpeers[k]))
        first.append(remote(mix_ref.at[:, right], mixing_ref.at[x, z, c, :, right], tsend.at[1, k], trecv.at[1, k], zpeers[k]))
        second.append(remote(mixing_ref.at[:, z, c, :, left], mixing_ref.at[:, z, c, :, left], tsend.at[2, k], trecv.at[2, k], zpeers[k]))
        second.append(remote(mixing_ref.at[x, :, c, :, right], mixing_ref.at[x, :, c, :, right], tsend.at[3, k], trecv.at[3, k], xpeers[k]))
    swap = remote(mixing_ref.at[:, :, c], mixing_ref.at[:, :, c], twin_send, twin_recv, twin)
    for copy in first:
        copy.start()
    mine = pltpu.make_async_copy(mix_ref, mixing_ref.at[x, z, c], own_sem.at[0])
    mine.start()
    mine.wait()
    load.wait()

    def copies(i, core):
        owner = NCORE * i + core
        cols = pl.ds(core * width, width)
        return (
            remote(means.at[i, :, cols], all_means_ref.at[me], msend.at[owner], mrecv.at[me], {"ens": owner}),
            remote(blocks.at[i, :, cols], out_ref.at[me], send.at[owner], recv.at[me], {"ens": owner}),
        )

    def localize(i):
        total = jnp.zeros((scen, tile), jnp.float32)
        for diag in range(diags):
            start = pl.multiple_of((i + diag) * tile, tile)
            prod = jnp.dot(padded[:, pl.ds(start, tile)], kernels_ref[diag], preferred_element_type=jnp.float32)
            total = total + prod * mask_ref[i, diag].astype(jnp.float32)
        mean = jnp.mean(total, axis=0, keepdims=True)
        means[i] = jnp.broadcast_to(mean, (8, tile))
        blocks[i] = (total - mean).astype(blocks.dtype)
        for core in range(NCORE):

            @pl.when(NCORE * i + core != me)
            def _():
                for copy in copies(i, core):
                    copy.start()

    each(0, inner, lambda n: localize(diags // 2 + (chip + 5 * n) % inner))
    for copy in first:
        copy.wait()
    for copy in second:
        copy.start()
    for copy in over_y:
        copy.wait()

    @pl.when(y == 0)
    def _():
        padded[:, 0:halo] = jnp.zeros((scen, halo), padded.dtype)

    @pl.when(y == NY - 1)
    def _():
        padded[:, halo + cells :] = jnp.zeros((scen, halo), padded.dtype)

    each(0, tiles - inner, lambda n: localize((inner + diags // 2 + (chip + n) % (tiles - inner)) % tiles))
    for copy in second:
        copy.wait()
    swap.start()

    own = (
        pltpu.make_async_copy(blocks.at[chip, :, pl.ds(pl.multiple_of(c * width, width), width)], out_ref.at[me], own_sem.at[0]),
        pltpu.make_async_copy(means.at[chip, :, pl.ds(pl.multiple_of(c * width, width), width)], all_means_ref.at[me], own_sem.at[1]),
    )
    for copy in own:
        copy.start()
    for copy in own:
        copy.wait()

    def finish(k):
        source = (me + k) % PLANE
        target = (me + PLANE - k) % PLANE
        tile_of, cols = target // NCORE, pl.ds(pl.multiple_of((target % NCORE) * width, width), width)
        remote(means.at[tile_of, :, cols], all_means_ref.at[source], msend.at[target], mrecv.at[source], {"ens": target}).wait()
        remote(blocks.at[tile_of, :, cols], out_ref.at[source], send.at[target], recv.at[source], {"ens": target}).wait()

    each(1, PLANE, finish)
    swap.wait()


def spread(snapshots, tile_mask, kernels, mix):
    scen, cells = snapshots.shape
    diags, tile, _ = kernels.shape
    tiles = cells // tile
    halo = (diags // 2) * tile
    width = cells // PLANE
    dma = pltpu.SemaphoreType.DMA
    return pl.pallas_call(
        spread_kernel,
        out_shape=(
            jax.ShapeDtypeStruct((PLANE, scen, width), jnp.bfloat16),
            jax.ShapeDtypeStruct((PLANE, 8, width), jnp.float32),
            jax.ShapeDtypeStruct((NX, NZ, NCORE) + mix.shape, mix.dtype),
        ),
        in_specs=[ANY, pl.BlockSpec(memory_space=pltpu.SMEM), VMEM, VMEM],
        out_specs=(VMEM, VMEM, VMEM),
        scratch_shapes=[
            pltpu.VMEM((scen, cells + 2 * halo), jnp.bfloat16),
            pltpu.VMEM((tiles, scen, tile), jnp.bfloat16),
            pltpu.VMEM((tiles, 8, tile), jnp.float32),
            dma, dma((2,)), dma((2,)), dma((2,)),
            dma((PLANE,)), dma((PLANE,)), dma((PLANE,)), dma((PLANE,)),
            dma((4, NX - 1)), dma((4, NX - 1)), dma, dma,
        ],
        compiler_params=pltpu.CompilerParams(collective_id=0, has_side_effects=True, vmem_limit_bytes=LIMIT),
        name="spread",
    )(snapshots, tile_mask, kernels, mix)


def gather_kernel(own_ref, out_ref, own_sem, send, recv, core_send, core_recv):
    me, x, z, c = place()
    half = own_ref.shape[1] // 2
    xs = [((x + k) % NX) for k in range(1, NX)]
    zs = [((z + k) % NZ) for k in range(1, NZ)]
    xpeers = [{"ens": v * NZ * NCORE + z * NCORE + c} for v in xs]
    zpeers = [{"ens": x * NZ * NCORE + v * NCORE + c} for v in zs]
    twin = {"ens": me + 1 - 2 * c}
    greet(xpeers + zpeers + [twin])
    left, right = pl.ds(0, half), pl.ds(half, half)
    first = []
    for k in range(NX - 1):
        first.append(remote(own_ref.at[:, left], out_ref.at[x, z, c, :, left], send.at[0, k], recv.at[0, k], xpeers[k]))
        first.append(remote(own_ref.at[:, right], out_ref.at[x, z, c, :, right], send.at[1, k], recv.at[1, k], zpeers[k]))
    for copy in first:
        copy.start()
    mine = pltpu.make_async_copy(own_ref, out_ref.at[x, z, c], own_sem)
    mine.start()
    mine.wait()
    for copy in first:
        copy.wait()
    second = []
    for k in range(NX - 1):
        second.append(remote(out_ref.at[:, z, c, :, left], out_ref.at[:, z, c, :, left], send.at[2, k], recv.at[2, k], zpeers[k]))
        second.append(remote(out_ref.at[x, :, c, :, right], out_ref.at[x, :, c, :, right], send.at[3, k], recv.at[3, k], xpeers[k]))
    for copy in second:
        copy.start()
    for copy in second:
        copy.wait()
    swap = remote(out_ref.at[:, :, c], out_ref.at[:, :, c], core_send, core_recv, twin)
    swap.start()
    swap.wait()


def gather(own, number):
    rows, cols = own.shape
    out = pl.pallas_call(
        gather_kernel,
        out_shape=jax.ShapeDtypeStruct((NX, NZ, NCORE, rows, cols), own.dtype),
        in_specs=[VMEM],
        out_specs=VMEM,
        scratch_shapes=[
            pltpu.SemaphoreType.DMA,
            pltpu.SemaphoreType.DMA((4, NX - 1)),
            pltpu.SemaphoreType.DMA((4, NX - 1)),
            pltpu.SemaphoreType.DMA,
            pltpu.SemaphoreType.DMA,
        ],
        compiler_params=pltpu.CompilerParams(collective_id=number, has_side_effects=True, vmem_limit_bytes=LIMIT),
        name="gather_rows",
    )(own)
    return out.reshape(PLANE * rows, cols)


def reduce_kernel(
    part_ref, gram_ref, rows_ref, out_gram_ref,
    from_twin, both, over_x, over_z, late_z, late_x, stage0, stage1, plane_sum, from_y,
    gram_in, gram_rows, gram_y,
    twin_send, twin_recv, send, recv, ysend, yrecv, gsend, grecv, gysend, gyrecv, bsend, brecv,
):
    me, x, z, c = place()
    y = lax.axis_index("grid")
    half = rows_ref.shape[1] // 2
    left, right = pl.ds(0, half), pl.ds(half, half)
    xs = [((x + k) % NX) for k in range(1, NX)]
    zs = [((z + k) % NZ) for k in range(1, NZ)]
    xpeers = [{"ens": v * NZ * NCORE + z * NCORE + c} for v in xs]
    zpeers = [{"ens": x * NZ * NCORE + v * NCORE + c} for v in zs]
    ypeers = [{"grid": (y + k) % NY} for k in range(1, NY)]
    twin = {"ens": me + 1 - 2 * c}
    greet_plane(me, ypeers)

    def gram_copy(k):
        peer = (me + k) % PLANE
        return remote(gram_ref.at[peer], gram_in.at[me], gsend.at[k], grecv.at[k], {"ens": peer})

    each(1, PLANE, lambda k: gram_copy(k).start())
    order = xs + [x]
    halves = [
        remote(part_ref.at[v, :, 1 - c], from_twin.at[v], twin_send.at[i], twin_recv.at[i], twin)
        for i, v in enumerate(order)
    ]
    for copy in halves:
        copy.start()
    x_first = []
    for i, v in enumerate(order):
        halves[i].wait()
        both[v] = part_ref[v, :, c] + from_twin[v]
        if i < NX - 1:
            copy = remote(both.at[v, :, :, left], over_x.at[i], send.at[0, i], recv.at[0, i], xpeers[i])
            copy.start()
            x_first.append(copy)
    z_first = []
    for i, v in enumerate(zs):
        copy = remote(both.at[:, v, :, right], over_z.at[i], send.at[1, i], recv.at[1, i], zpeers[i])
        copy.start()
        z_first.append(copy)
    gram_in[me] = gram_ref[me]
    each(1, PLANE, lambda k: gram_copy(k).wait())
    gram_rows[...] = jnp.sum(gram_in[...], axis=0)
    gram_over_y = [
        remote(gram_rows, gram_y.at[k], gysend.at[k], gyrecv.at[k], ypeers[k]) for k in range(NY - 1)
    ]
    for copy in gram_over_y:
        copy.start()
    for copy in gram_over_y:
        copy.wait()
    own_rows = gram_rows[...] + jnp.sum(gram_y[...], axis=0)
    out_gram_ref[me] = own_rows

    def gram_back(k):
        return remote(out_gram_ref.at[me], out_gram_ref.at[me], bsend.at[k], brecv.at[k], {"ens": (me + k) % PLANE})

    each(1, PLANE, lambda k: gram_back(k).start())
    for copy in x_first:
        copy.wait()
    stage0[...] = both[x, :, :, 0:half] + over_x[0] + over_x[1] + over_x[2]
    second = [
        remote(stage0.at[v], late_z.at[i], send.at[2, i], recv.at[2, i], zpeers[i]) for i, v in enumerate(zs)
    ]
    for copy in second:
        copy.start()
    for copy in z_first:
        copy.wait()
    stage1[...] = both[:, z, :, half:] + over_z[0] + over_z[1] + over_z[2]
    third = [
        remote(stage1.at[v], late_x.at[i], send.at[3, i], recv.at[3, i], xpeers[i]) for i, v in enumerate(xs)
    ]
    for copy in third:
        copy.start()
    for copy in second:
        copy.wait()
    plane_sum[:, 0:half] = stage0[z] + late_z[0] + late_z[1] + late_z[2]
    for copy in third:
        copy.wait()
    plane_sum[:, half:] = stage1[x] + late_x[0] + late_x[1] + late_x[2]
    over_y = [remote(plane_sum, from_y.at[k], ysend.at[k], yrecv.at[k], ypeers[k]) for k in range(NY - 1)]
    for copy in over_y:
        copy.start()
    for copy in over_y:
        copy.wait()
    rows_ref[...] = plane_sum[...] + from_y[0] + from_y[1] + from_y[2]
    each(1, PLANE, lambda k: gram_back(k).wait())


def reduce_sums(part, gram, number):
    total, cols = part.shape
    rows = total // PLANE
    half = cols // 2
    grows = gram.shape[0] // PLANE
    f32 = jnp.float32
    dma = pltpu.SemaphoreType.DMA
    out, summed = pl.pallas_call(
        reduce_kernel,
        out_shape=(
            jax.ShapeDtypeStruct((rows, cols), f32),
            jax.ShapeDtypeStruct((PLANE, grows, cols), f32),
        ),
        in_specs=[VMEM, VMEM],
        out_specs=(VMEM, VMEM),
        scratch_shapes=[
            pltpu.VMEM((NX, NZ, rows, cols), f32),
            pltpu.VMEM((NX, NZ, rows, cols), f32),
            pltpu.VMEM((NX - 1, NZ, rows, half), f32),
            pltpu.VMEM((NZ - 1, NX, rows, half), f32),
            pltpu.VMEM((NZ - 1, rows, half), f32),
            pltpu.VMEM((NX - 1, rows, half), f32),
            pltpu.VMEM((NZ, rows, half), f32),
            pltpu.VMEM((NX, rows, half), f32),
            pltpu.VMEM((rows, cols), f32),
            pltpu.VMEM((NY - 1, rows, cols), f32),
            pltpu.VMEM((PLANE, grows, cols), f32),
            pltpu.VMEM((grows, cols), f32),
            pltpu.VMEM((NY - 1, grows, cols), f32),
            dma((NX,)), dma((NX,)), dma((4, NX - 1)), dma((4, NX - 1)), dma((NY - 1,)), dma((NY - 1,)),
            dma((PLANE,)), dma((PLANE,)), dma((NY - 1,)), dma((NY - 1,)), dma((PLANE,)), dma((PLANE,)),
        ],
        compiler_params=pltpu.CompilerParams(collective_id=number, has_side_effects=True, vmem_limit_bytes=LIMIT),
        name="reduce_sums",
    )(part.reshape(NX, NZ, NCORE, rows, cols), gram.reshape(PLANE, grows, cols))
    return out, summed.reshape(gram.shape)


BLOCK = 64


def eliminated(m):
    size = m.shape[0]
    row = lax.broadcasted_iota(jnp.int32, m.shape, 0)
    col = lax.broadcasted_iota(jnp.int32, m.shape, 1)
    for j in range(0, size, 2):
        c0 = jnp.broadcast_to(m[:, j : j + 1], m.shape)
        c1 = jnp.broadcast_to(m[:, j + 1 : j + 2], m.shape)
        r0 = m[j : j + 1, :]
        r1 = m[j + 1 : j + 2, :]
        d0 = c0[j : j + 1, :]
        e = c0[j + 1 : j + 2, :]
        f = c1[j + 1 : j + 2, :]
        ratio = e / d0
        d1 = f - e * ratio
        u0 = r0 / d0
        u1 = (r1 - ratio * r0) / d1
        c1 = jnp.where(row > j + 1, c1 - c0 * ratio, 0.0)
        c0 = jnp.where(row > j, c0, 0.0)
        m = m - c0 * u0 - c1 * u1
    diag = jnp.sum(jnp.where(row == col, m, 0.0), axis=1, keepdims=True)
    return m * (1.0 / jnp.sqrt(diag))


def inverse_factor_kernel(gram_ref, out_ref, work):
    n = gram_ref.shape[0]
    work[:, 0:n] = gram_ref[...]
    row = lax.broadcasted_iota(jnp.int32, (n, n), 0)
    col = lax.broadcasted_iota(jnp.int32, (n, n), 1)
    work[:, n:] = jnp.where(row == col, 1.0, 0.0)
    brow = lax.broadcasted_iota(jnp.int32, (BLOCK, BLOCK), 0)
    bcol = lax.broadcasted_iota(jnp.int32, (BLOCK, BLOCK), 1)
    unit = jnp.where(brow == bcol, 1.0, 0.0)
    for low in range(0, n, BLOCK):
        high = low + BLOCK
        block = work[low:high, low:high]
        inv = eliminated(jnp.concatenate([block, unit], axis=1))[:, BLOCK:]
        scaled = jnp.dot(inv, work[low:high, :], precision=HIGHEST, preferred_element_type=jnp.float32)
        out_ref[low:high, :] = scaled[:, n:]
        if high < n:
            lower = scaled[:, high:n]
            update = lax.dot_general(
                lower, scaled, (((0,), (0,)), ((), ())), precision=HIGHEST, preferred_element_type=jnp.float32
            )
            work[high:, :] = work[high:, :] - update


def inverse_factor(gram):
    n = gram.shape[0]
    return pl.pallas_call(
        inverse_factor_kernel,
        out_shape=jax.ShapeDtypeStruct((n, n), jnp.float32),
        in_specs=[VMEM],
        out_specs=VMEM,
        scratch_shapes=[pltpu.VMEM((n, 2 * n), jnp.float32)],
        name="inverse_factor",
    )(gram)


def product(fields, span):
    high = span.astype(jnp.bfloat16)
    low = (span - high.astype(jnp.float32)).astype(jnp.bfloat16)
    both = jnp.dot(fields, jnp.concatenate([high, low], axis=1), preferred_element_type=jnp.float32)
    cols = span.shape[1]
    return both[:, :cols] + both[:, cols:]


def span_of(fields, mixing):
    return lax.dot_general(fields, mixing, (((0,), (0,)), ((), ())), preferred_element_type=jnp.float32)


def gram_of(span):
    return lax.dot_general(span, span, (((0,), (0,)), ((), ())), precision=HIGHEST)


def times_inverse_transposed(rows, inverse):
    return lax.dot_general(rows, inverse, (((1,), (1,)), ((), ())), precision=HIGHEST)


def per_device(snapshots, tile_mask, kernels, test_matrix):
    total_cells = snapshots.shape[1] * lax.axis_size("grid")
    rank_width = test_matrix.shape[1]
    blocks, all_means, mixing = spread(snapshots, tile_mask, kernels, test_matrix)
    mixing = mixing.reshape(-1, rank_width)
    all_means = all_means[:, :1]
    shift = all_means - jnp.mean(all_means, axis=0, keepdims=True)
    fields = (blocks.astype(jnp.float32) + shift).astype(jnp.bfloat16)
    fields = fields.reshape(-1, fields.shape[2])

    first_span = span_of(fields, mixing)
    rows, gram = reduce_sums(product(fields, first_span), gram_of(first_span), 2)
    weights = times_inverse_transposed(rows, inverse_factor(gram)).astype(jnp.bfloat16)
    second_span = span_of(fields, gather(weights, 3))
    rows, gram = reduce_sums(product(fields, second_span), gram_of(second_span), 4)
    inverse = inverse_factor(gram)
    basis = times_inverse_transposed(second_span, inverse) * math.sqrt(total_cells)
    coefficients = times_inverse_transposed(rows, inverse) * math.sqrt(rank_width / total_cells)
    return (basis, coefficients)


def solution(mesh):
    return jax.shard_map(
        per_device,
        mesh=mesh,
        in_specs=(P("ens", "grid"), P("grid", None), P(), P("ens", None)),
        out_specs=(P(("grid", "ens"), None), P("ens", None)),
        check_vma=False,
    )
```

```python
import functools
import math

import jax
import jax.numpy as jnp
from jax import lax
from jax.experimental import pallas as pl
from jax.experimental.pallas import tpu as pltpu
from jax.sharding import PartitionSpec as P

MESH = pl.DeviceIdType.MESH
HIGHEST = lax.Precision.HIGHEST
VMEM = pl.BlockSpec(memory_space=pltpu.VMEM)
ANY = pl.BlockSpec(memory_space=pl.ANY)
NX, NZ, NCORE, NY = 4, 4, 2, 4
PLANE = NX * NZ * NCORE
LIMIT = 60 * 1024 * 1024


def place():
    me = lax.axis_index("ens")
    return me, me // (NZ * NCORE), (me // NCORE) % NZ, me % NCORE


def greet(peers):
    barrier = pltpu.get_barrier_semaphore()
    for peer in peers:
        pl.semaphore_signal(barrier, inc=1, device_id=peer, device_id_type=MESH)
    pl.semaphore_wait(barrier, len(peers))


def greet_plane(me, others=()):
    barrier = pltpu.get_barrier_semaphore()

    def one(k, carry):
        peer = (me + k) % PLANE
        pl.semaphore_signal(barrier, inc=1, device_id={"ens": peer}, device_id_type=MESH)
        return carry

    lax.fori_loop(1, PLANE, one, 0)
    for peer in others:
        pl.semaphore_signal(barrier, inc=1, device_id=peer, device_id_type=MESH)
    pl.semaphore_wait(barrier, PLANE - 1 + len(others))


def remote(src, dst, send, recv, peer):
    return pltpu.make_async_remote_copy(
        src_ref=src, dst_ref=dst, send_sem=send, recv_sem=recv, device_id=peer, device_id_type=MESH
    )


def each(low, high, body):
    def step(k, carry):
        body(k)
        return carry

    lax.fori_loop(low, high, step, 0)


def spread_kernel(
    snap_ref, mask_ref, kernels_ref, mix_ref,
    out_ref, all_means_ref, mixing_ref,
    padded, blocks, means,
    load_sem, own_sem, hsend, hrecv, send, recv, msend, mrecv, tsend, trecv, twin_send, twin_recv,
):
    me, x, z, c = place()
    y = lax.axis_index("grid")
    chip = me // NCORE
    diags, tile, _ = kernels_ref.shape
    halo = (diags // 2) * tile
    scen, cells = snap_ref.shape
    tiles = cells // tile
    width = out_ref.shape[2]
    inner = tiles - 2 * (diags // 2)
    up, down = {"grid": (y + 1) % NY}, {"grid": (y + NY - 1) % NY}
    greet_plane(me, (up, down))

    load = pltpu.make_async_copy(snap_ref, padded.at[:, pl.ds(halo, cells)], load_sem)
    load.start()
    over_y = (
        remote(snap_ref.at[:, pl.ds(cells - halo, halo)], padded.at[:, pl.ds(0, halo)], hsend.at[0], hrecv.at[0], up),
        remote(snap_ref.at[:, pl.ds(0, halo)], padded.at[:, pl.ds(halo + cells, halo)], hsend.at[1], hrecv.at[1], down),
    )
    for copy in over_y:
        copy.start()

    half = mix_ref.shape[1] // 2
    left, right = pl.ds(0, half), pl.ds(half, half)
    xpeers = [{"ens": ((x + k) % NX) * NZ * NCORE + z * NCORE + c} for k in range(1, NX)]
    zpeers = [{"ens": x * NZ * NCORE + ((z + k) % NZ) * NCORE + c} for k in range(1, NZ)]
    twin = {"ens": me + 1 - 2 * c}
    first, second = [], []
    for k in range(NX - 1):
        first.append(remote(mix_ref.at[:, left], mixing_ref.at[x, z, c, :, left], tsend.at[0, k], trecv.at[0, k], xpeers[k]))
        first.append(remote(mix_ref.at[:, right], mixing_ref.at[x, z, c, :, right], tsend.at[1, k], trecv.at[1, k], zpeers[k]))
        second.append(remote(mixing_ref.at[:, z, c, :, left], mixing_ref.at[:, z, c, :, left], tsend.at[2, k], trecv.at[2, k], zpeers[k]))
        second.append(remote(mixing_ref.at[x, :, c, :, right], mixing_ref.at[x, :, c, :, right], tsend.at[3, k], trecv.at[3, k], xpeers[k]))
    swap = remote(mixing_ref.at[:, :, c], mixing_ref.at[:, :, c], twin_send, twin_recv, twin)
    for copy in first:
        copy.start()
    mine = pltpu.make_async_copy(mix_ref, mixing_ref.at[x, z, c], own_sem.at[0])
    mine.start()
    mine.wait()
    load.wait()

    def copies(i, core):
        owner = NCORE * i + core
        cols = pl.ds(core * width, width)
        return (
            remote(means.at[i, :, cols], all_means_ref.at[me], msend.at[owner], mrecv.at[me], {"ens": owner}),
            remote(blocks.at[i, :, cols], out_ref.at[me], send.at[owner], recv.at[me], {"ens": owner}),
        )

    def localize(i):
        total = jnp.zeros((scen, tile), jnp.float32)
        for diag in range(diags):
            start = pl.multiple_of((i + diag) * tile, tile)
            prod = jnp.dot(padded[:, pl.ds(start, tile)], kernels_ref[diag], preferred_element_type=jnp.float32)
            total = total + prod * mask_ref[i, diag].astype(jnp.float32)
        mean = jnp.mean(total, axis=0, keepdims=True)
        means[i] = jnp.broadcast_to(mean, (8, tile))
        blocks[i] = (total - mean).astype(blocks.dtype)
        for core in range(NCORE):

            @pl.when(NCORE * i + core != me)
            def _():
                for copy in copies(i, core):
                    copy.start()

    each(0, inner, lambda n: localize(diags // 2 + (chip + 5 * n) % inner))
    for copy in first:
        copy.wait()
    for copy in second:
        copy.start()
    for copy in over_y:
        copy.wait()

    @pl.when(y == 0)
    def _():
        padded[:, 0:halo] = jnp.zeros((scen, halo), padded.dtype)

    @pl.when(y == NY - 1)
    def _():
        padded[:, halo + cells :] = jnp.zeros((scen, halo), padded.dtype)

    each(0, tiles - inner, lambda n: localize((inner + diags // 2 + (chip + n) % (tiles - inner)) % tiles))
    for copy in second:
        copy.wait()
    swap.start()

    own = (
        pltpu.make_async_copy(blocks.at[chip, :, pl.ds(pl.multiple_of(c * width, width), width)], out_ref.at[me], own_sem.at[0]),
        pltpu.make_async_copy(means.at[chip, :, pl.ds(pl.multiple_of(c * width, width), width)], all_means_ref.at[me], own_sem.at[1]),
    )
    for copy in own:
        copy.start()
    for copy in own:
        copy.wait()

    def finish(k):
        source = (me + k) % PLANE
        target = (me + PLANE - k) % PLANE
        tile_of, cols = target // NCORE, pl.ds(pl.multiple_of((target % NCORE) * width, width), width)
        remote(means.at[tile_of, :, cols], all_means_ref.at[source], msend.at[target], mrecv.at[source], {"ens": target}).wait()
        remote(blocks.at[tile_of, :, cols], out_ref.at[source], send.at[target], recv.at[source], {"ens": target}).wait()

    each(1, PLANE, finish)
    swap.wait()


def spread(snapshots, tile_mask, kernels, mix):
    scen, cells = snapshots.shape
    diags, tile, _ = kernels.shape
    tiles = cells // tile
    halo = (diags // 2) * tile
    width = cells // PLANE
    dma = pltpu.SemaphoreType.DMA
    return pl.pallas_call(
        spread_kernel,
        out_shape=(
            jax.ShapeDtypeStruct((PLANE, scen, width), jnp.bfloat16),
            jax.ShapeDtypeStruct((PLANE, 8, width), jnp.float32),
            jax.ShapeDtypeStruct((NX, NZ, NCORE) + mix.shape, mix.dtype),
        ),
        in_specs=[ANY, pl.BlockSpec(memory_space=pltpu.SMEM), VMEM, VMEM],
        out_specs=(VMEM, VMEM, VMEM),
        scratch_shapes=[
            pltpu.VMEM((scen, cells + 2 * halo), jnp.bfloat16),
            pltpu.VMEM((tiles, scen, tile), jnp.bfloat16),
            pltpu.VMEM((tiles, 8, tile), jnp.float32),
            dma, dma((2,)), dma((2,)), dma((2,)),
            dma((PLANE,)), dma((PLANE,)), dma((PLANE,)), dma((PLANE,)),
            dma((4, NX - 1)), dma((4, NX - 1)), dma, dma,
        ],
        compiler_params=pltpu.CompilerParams(collective_id=0, has_side_effects=True, vmem_limit_bytes=LIMIT),
        name="spread",
    )(snapshots, tile_mask, kernels, mix)


def gather_kernel(own_ref, out_ref, own_sem, send, recv, core_send, core_recv):
    me, x, z, c = place()
    half = own_ref.shape[1] // 2
    xs = [((x + k) % NX) for k in range(1, NX)]
    zs = [((z + k) % NZ) for k in range(1, NZ)]
    xpeers = [{"ens": v * NZ * NCORE + z * NCORE + c} for v in xs]
    zpeers = [{"ens": x * NZ * NCORE + v * NCORE + c} for v in zs]
    twin = {"ens": me + 1 - 2 * c}
    greet(xpeers + zpeers + [twin])
    left, right = pl.ds(0, half), pl.ds(half, half)
    first = []
    for k in range(NX - 1):
        first.append(remote(own_ref.at[:, left], out_ref.at[x, z, c, :, left], send.at[0, k], recv.at[0, k], xpeers[k]))
        first.append(remote(own_ref.at[:, right], out_ref.at[x, z, c, :, right], send.at[1, k], recv.at[1, k], zpeers[k]))
    for copy in first:
        copy.start()
    mine = pltpu.make_async_copy(own_ref, out_ref.at[x, z, c], own_sem)
    mine.start()
    mine.wait()
    for copy in first:
        copy.wait()
    second = []
    for k in range(NX - 1):
        second.append(remote(out_ref.at[:, z, c, :, left], out_ref.at[:, z, c, :, left], send.at[2, k], recv.at[2, k], zpeers[k]))
        second.append(remote(out_ref.at[x, :, c, :, right], out_ref.at[x, :, c, :, right], send.at[3, k], recv.at[3, k], xpeers[k]))
    for copy in second:
        copy.start()
    for copy in second:
        copy.wait()
    swap = remote(out_ref.at[:, :, c], out_ref.at[:, :, c], core_send, core_recv, twin)
    swap.start()
    swap.wait()


def gather(own, number):
    rows, cols = own.shape
    out = pl.pallas_call(
        gather_kernel,
        out_shape=jax.ShapeDtypeStruct((NX, NZ, NCORE, rows, cols), own.dtype),
        in_specs=[VMEM],
        out_specs=VMEM,
        scratch_shapes=[
            pltpu.SemaphoreType.DMA,
            pltpu.SemaphoreType.DMA((4, NX - 1)),
            pltpu.SemaphoreType.DMA((4, NX - 1)),
            pltpu.SemaphoreType.DMA,
            pltpu.SemaphoreType.DMA,
        ],
        compiler_params=pltpu.CompilerParams(collective_id=number, has_side_effects=True, vmem_limit_bytes=LIMIT),
        name="gather_rows",
    )(own)
    return out.reshape(PLANE * rows, cols)


BLOCK = 64


def eliminated(m):
    size = m.shape[0]
    row = lax.broadcasted_iota(jnp.int32, m.shape, 0)
    col = lax.broadcasted_iota(jnp.int32, m.shape, 1)
    for j in range(0, size, 2):
        c0 = jnp.broadcast_to(m[:, j : j + 1], m.shape)
        c1 = jnp.broadcast_to(m[:, j + 1 : j + 2], m.shape)
        r0 = m[j : j + 1, :]
        r1 = m[j + 1 : j + 2, :]
        d0 = c0[j : j + 1, :]
        e = c0[j + 1 : j + 2, :]
        f = c1[j + 1 : j + 2, :]
        ratio = e / d0
        d1 = f - e * ratio
        u0 = r0 / d0
        u1 = (r1 - ratio * r0) / d1
        c1 = jnp.where(row > j + 1, c1 - c0 * ratio, 0.0)
        c0 = jnp.where(row > j, c0, 0.0)
        m = m - c0 * u0 - c1 * u1
    diag = jnp.sum(jnp.where(row == col, m, 0.0), axis=1, keepdims=True)
    return m * (1.0 / jnp.sqrt(diag))


def factor_start(gram, work):
    n = gram.shape[0]
    work[:, 0:n] = gram
    row = lax.broadcasted_iota(jnp.int32, (n, n), 0)
    col = lax.broadcasted_iota(jnp.int32, (n, n), 1)
    work[:, n:] = jnp.where(row == col, 1.0, 0.0)


def factor_block(low, work, out_ref):
    n = out_ref.shape[0]
    high = low + BLOCK
    brow = lax.broadcasted_iota(jnp.int32, (BLOCK, BLOCK), 0)
    bcol = lax.broadcasted_iota(jnp.int32, (BLOCK, BLOCK), 1)
    unit = jnp.where(brow == bcol, 1.0, 0.0)
    block = work[low:high, low:high]
    inv = eliminated(jnp.concatenate([block, unit], axis=1))[:, BLOCK:]
    scaled = jnp.dot(inv, work[low:high, :], precision=HIGHEST, preferred_element_type=jnp.float32)
    out_ref[low:high, :] = scaled[:, n:]
    if high < n:
        lower = scaled[:, high:n]
        update = lax.dot_general(
            lower, scaled, (((0,), (0,)), ((), ())), precision=HIGHEST, preferred_element_type=jnp.float32
        )
        work[high:, :] = work[high:, :] - update


def reduce_kernel(
    part_ref, gram_ref, rows_ref, inverse_ref,
    from_twin, both, over_x, over_z, late_z, late_x, stage0, stage1, plane_sum, from_y,
    gram_in, gram_rows, gram_y, out_gram_ref, work,
    twin_send, twin_recv, send, recv, ysend, yrecv, gsend, grecv, gysend, gyrecv, bsend, brecv,
):
    me, x, z, c = place()
    y = lax.axis_index("grid")
    half = rows_ref.shape[1] // 2
    left, right = pl.ds(0, half), pl.ds(half, half)
    xs = [((x + k) % NX) for k in range(1, NX)]
    zs = [((z + k) % NZ) for k in range(1, NZ)]
    xpeers = [{"ens": v * NZ * NCORE + z * NCORE + c} for v in xs]
    zpeers = [{"ens": x * NZ * NCORE + v * NCORE + c} for v in zs]
    ypeers = [{"grid": (y + k) % NY} for k in range(1, NY)]
    twin = {"ens": me + 1 - 2 * c}
    greet_plane(me, ypeers)

    def gram_copy(k):
        peer = (me + k) % PLANE
        return remote(gram_ref.at[peer], gram_in.at[me], gsend.at[k], grecv.at[k], {"ens": peer})

    each(1, PLANE, lambda k: gram_copy(k).start())
    order = xs + [x]
    halves = [
        remote(part_ref.at[v, :, 1 - c], from_twin.at[v], twin_send.at[i], twin_recv.at[i], twin)
        for i, v in enumerate(order)
    ]
    for copy in halves:
        copy.start()
    gram_in[me] = gram_ref[me]
    each(1, PLANE, lambda k: gram_copy(k).wait())
    gram_rows[...] = jnp.sum(gram_in[...], axis=0)
    gram_over_y = [
        remote(gram_rows, gram_y.at[y], gysend.at[k], gyrecv.at[k], ypeers[k]) for k in range(NY - 1)
    ]
    for copy in gram_over_y:
        copy.start()
    for copy in gram_over_y:
        copy.wait()
    gram_y[y] = gram_rows[...]
    out_gram_ref[me] = jnp.sum(gram_y[...], axis=0)

    def gram_back(k):
        return remote(out_gram_ref.at[me], out_gram_ref.at[me], bsend.at[k], brecv.at[k], {"ens": (me + k) % PLANE})

    each(1, PLANE, lambda k: gram_back(k).start())
    x_first = []
    for i, v in enumerate(order):
        halves[i].wait()
        both[v] = part_ref[v, :, c] + from_twin[v]
        if i < NX - 1:
            copy = remote(both.at[v, :, :, left], over_x.at[i], send.at[0, i], recv.at[0, i], xpeers[i])
            copy.start()
            x_first.append(copy)
    z_first = []
    for i, v in enumerate(zs):
        copy = remote(both.at[:, v, :, right], over_z.at[i], send.at[1, i], recv.at[1, i], zpeers[i])
        copy.start()
        z_first.append(copy)
    each(1, PLANE, lambda k: gram_back(k).wait())
    n = inverse_ref.shape[0]
    factor_start(out_gram_ref[...].reshape(n, n), work)
    factor_block(0, work, inverse_ref)
    factor_block(BLOCK, work, inverse_ref)
    for copy in x_first:
        copy.wait()
    stage0[...] = both[x, :, :, 0:half] + over_x[0] + over_x[1] + over_x[2]
    second = [
        remote(stage0.at[v], late_z.at[i], send.at[2, i], recv.at[2, i], zpeers[i]) for i, v in enumerate(zs)
    ]
    for copy in second:
        copy.start()
    for copy in z_first:
        copy.wait()
    stage1[...] = both[:, z, :, half:] + over_z[0] + over_z[1] + over_z[2]
    third = [
        remote(stage1.at[v], late_x.at[i], send.at[3, i], recv.at[3, i], xpeers[i]) for i, v in enumerate(xs)
    ]
    for copy in third:
        copy.start()
    factor_block(2 * BLOCK, work, inverse_ref)
    for copy in second:
        copy.wait()
    plane_sum[:, 0:half] = stage0[z] + late_z[0] + late_z[1] + late_z[2]
    for copy in third:
        copy.wait()
    plane_sum[:, half:] = stage1[x] + late_x[0] + late_x[1] + late_x[2]
    over_y = [remote(plane_sum, from_y.at[y], ysend.at[k], yrecv.at[k], ypeers[k]) for k in range(NY - 1)]
    for copy in over_y:
        copy.start()
    factor_block(3 * BLOCK, work, inverse_ref)
    for copy in over_y:
        copy.wait()
    from_y[y] = plane_sum[...]
    rows_ref[...] = jnp.sum(from_y[...], axis=0)


def reduce_sums(part, gram, number):
    total, cols = part.shape
    rows = total // PLANE
    half = cols // 2
    grows = gram.shape[0] // PLANE
    f32 = jnp.float32
    dma = pltpu.SemaphoreType.DMA
    return pl.pallas_call(
        reduce_kernel,
        out_shape=(
            jax.ShapeDtypeStruct((rows, cols), f32),
            jax.ShapeDtypeStruct(gram.shape, f32),
        ),
        in_specs=[VMEM, VMEM],
        out_specs=(VMEM, VMEM),
        scratch_shapes=[
            pltpu.VMEM((NX, NZ, rows, cols), f32),
            pltpu.VMEM((NX, NZ, rows, cols), f32),
            pltpu.VMEM((NX - 1, NZ, rows, half), f32),
            pltpu.VMEM((NZ - 1, NX, rows, half), f32),
            pltpu.VMEM((NZ - 1, rows, half), f32),
            pltpu.VMEM((NX - 1, rows, half), f32),
            pltpu.VMEM((NZ, rows, half), f32),
            pltpu.VMEM((NX, rows, half), f32),
            pltpu.VMEM((rows, cols), f32),
            pltpu.VMEM((NY, rows, cols), f32),
            pltpu.VMEM((PLANE, grows, cols), f32),
            pltpu.VMEM((grows, cols), f32),
            pltpu.VMEM((NY, grows, cols), f32),
            pltpu.VMEM((PLANE, grows, cols), f32),
            pltpu.VMEM((gram.shape[0], 2 * gram.shape[0]), f32),
            dma((NX,)), dma((NX,)), dma((4, NX - 1)), dma((4, NX - 1)), dma((NY - 1,)), dma((NY - 1,)),
            dma((PLANE,)), dma((PLANE,)), dma((NY - 1,)), dma((NY - 1,)), dma((PLANE,)), dma((PLANE,)),
        ],
        compiler_params=pltpu.CompilerParams(collective_id=number, has_side_effects=True, vmem_limit_bytes=LIMIT),
        name="reduce_sums",
    )(part.reshape(NX, NZ, NCORE, rows, cols), gram.reshape(PLANE, grows, cols))


def product(fields, span):
    high = span.astype(jnp.bfloat16)
    low = (span - high.astype(jnp.float32)).astype(jnp.bfloat16)
    both = jnp.dot(fields, jnp.concatenate([high, low], axis=1), preferred_element_type=jnp.float32)
    cols = span.shape[1]
    return both[:, :cols] + both[:, cols:]


def span_of(fields, mixing):
    return lax.dot_general(fields, mixing, (((0,), (0,)), ((), ())), preferred_element_type=jnp.float32)


def gram_of(span):
    return lax.dot_general(span, span, (((0,), (0,)), ((), ())), precision=HIGHEST)


def times_inverse_transposed(rows, inverse):
    return lax.dot_general(rows, inverse, (((1,), (1,)), ((), ())), precision=HIGHEST)


def per_device(snapshots, tile_mask, kernels, test_matrix):
    total_cells = snapshots.shape[1] * lax.axis_size("grid")
    rank_width = test_matrix.shape[1]
    blocks, all_means, mixing = spread(snapshots, tile_mask, kernels, test_matrix)
    mixing = mixing.reshape(-1, rank_width)
    all_means = all_means[:, :1]
    shift = all_means - jnp.mean(all_means, axis=0, keepdims=True)
    fields = (blocks.astype(jnp.float32) + shift).astype(jnp.bfloat16)
    fields = fields.reshape(-1, fields.shape[2])

    first_span = span_of(fields, mixing)
    rows, inverse = reduce_sums(product(fields, first_span), gram_of(first_span), 2)
    weights = times_inverse_transposed(rows, inverse).astype(jnp.bfloat16)
    second_span = span_of(fields, gather(weights, 3))
    rows, inverse = reduce_sums(product(fields, second_span), gram_of(second_span), 4)
    basis = times_inverse_transposed(second_span, inverse) * math.sqrt(total_cells)
    coefficients = times_inverse_transposed(rows, inverse) * math.sqrt(rank_width / total_cells)
    return (basis, coefficients)


def solution(mesh):
    return jax.shard_map(
        per_device,
        mesh=mesh,
        in_specs=(P("ens", "grid"), P("grid", None), P(), P("ens", None)),
        out_specs=(P(("grid", "ens"), None), P("ens", None)),
        check_vma=False,
    )
```
